128 devices in a mesh: lon: 16 (over y_lo, x, core), lat: 8 (over z, y_hi).
Axes of the slice: x: 4, y: 4 (y_hi: 2, y_lo: 2; y = y_hi * 2 + y_lo), z: 4, core: 2. Of those that a mesh axis runs over, the one named last changes fastest.
Arguments:
- terminal_error_derivative: float32 [4, 48, 512, 2048], P(None, None, 'lat', 'lon'), may hold values from -6 to 6
- trajectory_advective_shift: float32 [2, 2, 48, 512, 2048], P(None, None, None, 'lat', 'lon'), may hold values from -1 to 1
- layer_interaction_matrix: float32 [48, 4, 4], replicated, may hold values from -1.2 to 1.2
- measured_local_profile_slot: int32 [128, 16, 256], P(('lon', 'lat')), may hold values from 0 to 8191
- measured_active_tally: int32 [128, 16], P(('lon', 'lat')), may hold values from 0 to 256, as said below
- measurement_operator_matrix: bfloat16 [128, 16, 192, 256], P(('lon', 'lat')), may hold values from -0.4375 to 0.4375
- measured_departure_values: float32 [128, 16, 256], P(('lon', 'lat')), may hold values from -5 to 5
Outputs:
- analysis_sens: float32 [4, 48, 512, 2048], P(None, None, 'lat', 'lon')
- obs_impact: float32 [128, 16, 256], P(('lon', 'lat'))
The draws below stay inside these ranges and needn't reach their ends.
Inputs may be any that keep to these rules, and one draw needn't show every extreme that they name: `measured_active_tally`: entry [s, k] counts the live slots of device s's list for sector k; slots from it on are padding. In every draw some list is full with 256 entries.
All inputs are finite; a program needn't handle non-finite values.
Results may differ from the reference program's by a relative error of at most 0.0005.
Values may be sent and summed in bfloat16 or wider, within the bound.
A program may use at most 192 MiB of HBM per device.

```python
import jax
import jax.numpy as jnp
from jax import lax

PROGNOSTIC_TOTAL = 4
VERTICAL_LAYERS = 48
CLAT = 64
CLON = 128
CAP = 256
PARALLEL_BANDS = 512
MERIDIAN_SLOTS = 2048
N_LON = 16
N_LAT = 8


def draw_measured_active_tally(key, part):
    keys = jax.random.split(key, 5)
    total_rows = N_LON * N_LAT
    offset = jax.random.randint(keys[0], (), 0, 4)
    band = jnp.arange(total_rows, dtype=jnp.int32)[:, None] % N_LAT
    sector = jnp.arange(N_LON, dtype=jnp.int32)[None, :]
    swath = (sector + band + offset) % 4 == 0
    busy = jax.random.randint(keys[1], (total_rows, N_LON), CAP // 2, CAP + 1)
    quiet = jax.random.randint(keys[2], (total_rows, N_LON), CAP // 16, CAP // 4 + 1)
    counts = jnp.where(swath, busy, quiet)
    which_row = jax.random.randint(keys[3], (), 0, total_rows)
    which_col = jax.random.randint(keys[4], (), 0, N_LON)
    return counts.at[which_row, which_col].set(CAP).astype(jnp.int32)


def with_ends(result, stream_key, smallest, top_value):
    place = [jax.random.randint(jax.random.fold_in(stream_key, axis), (), 0, length) for axis, length in enumerate(result.shape)]
    widest = result.shape.index(max(result.shape))
    neighbour = place[:widest] + [(place[widest] + 1) % result.shape[widest]] + place[widest + 1:]
    return result.at[tuple(place)].set(smallest).at[tuple(neighbour)].set(top_value)


def steps_of(own_key, shape, cuts, smallest, top_value):
    def one(axis_at, parts):
        steps = jax.random.uniform(jax.random.fold_in(jax.random.fold_in(own_key, 6), axis_at), (parts,), jnp.float32, smallest / len(cuts), top_value / len(cuts))
        return jnp.repeat(jnp.exp(steps), shape[axis_at] // parts).reshape((-1,) + (1,) * (len(shape) - axis_at - 1))

    loudness = one(*cuts[0])
    for cut in cuts[1:]:
        loudness = loudness * one(*cut)
    return loudness


def scatter_about(own_key, dims, width, most, shards=(), kind=jnp.bfloat16):
    values = width * jax.random.normal(own_key, dims, jnp.float32)
    if shards:
        values = values * steps_of(own_key, dims, shards, -0.22, 0.18)
    return jnp.clip(values, -most, most).astype(kind)


def setup_inputs(seed: int = 0) -> dict:
    key_list = jax.random.split(jax.random.key(seed), 8)
    terminal_error_derivative = scatter_about(key_list[0], (PROGNOSTIC_TOTAL, VERTICAL_LAYERS, PARALLEL_BANDS, MERIDIAN_SLOTS), 1.0, 6.0, ((2, 8), (3, 16)), jnp.float32)
    trajectory_advective_shift = scatter_about(key_list[1], (2, 2, VERTICAL_LAYERS, PARALLEL_BANDS, MERIDIAN_SLOTS), 0.25, 1.0, ((3, 8), (4, 16)), jnp.float32)
    layer_interaction_matrix = scatter_about(key_list[2], (VERTICAL_LAYERS, PROGNOSTIC_TOTAL, PROGNOSTIC_TOTAL), 0.3, 1.2, (), jnp.float32)
    measured_local_profile_slot = with_ends(jax.random.randint(key_list[3], (N_LON * N_LAT, N_LON, CAP), 0, CLAT * CLON), jax.random.fold_in(key_list[3], 1), 0, (CLAT * CLON) - 1).astype(jnp.int32)
    measured_active_tally = draw_measured_active_tally(jax.random.fold_in(key_list[7], 71), 0)
    measurement_operator_matrix = scatter_about(key_list[5], (N_LON * N_LAT, N_LON, PROGNOSTIC_TOTAL * VERTICAL_LAYERS, CAP), (PROGNOSTIC_TOTAL * VERTICAL_LAYERS) ** -0.5, 0.4375, ((0, 128),))
    measured_departure_values = scatter_about(key_list[6], (N_LON * N_LAT, N_LON, CAP), 1.0, 5.0, ((0, 128),), jnp.float32)
    return {"terminal_error_derivative": terminal_error_derivative, "trajectory_advective_shift": trajectory_advective_shift, "layer_interaction_matrix": layer_interaction_matrix, "measured_local_profile_slot": measured_local_profile_slot, "measured_active_tally": measured_active_tally, "measurement_operator_matrix": measurement_operator_matrix, "measured_departure_values": measured_departure_values}


def adjoint_level(prognostic_variable_slot, along, across, coupling_level):
    lon_prod = along[None] * prognostic_variable_slot
    lat_prod = across[None] * prognostic_variable_slot
    lon_term = jnp.roll(lon_prod, 1, axis=2) - jnp.roll(lon_prod, -1, axis=2)
    padded = jnp.pad(lat_prod, ((0, 0), (1, 1), (0, 0)))
    lat_term = padded[:, :-2] - padded[:, 2:]
    coupled = jnp.einsum("ef,eab->fab", coupling_level, prognostic_variable_slot, precision=lax.Precision.HIGHEST)
    return prognostic_variable_slot + coupled - lon_term - lat_term


def vertical_layer_traversal(inputs):
    prognostic_variable_slot, winds, coupling_level = inputs
    middle = adjoint_level(prognostic_variable_slot, winds[1, 0], winds[1, 1], coupling_level)
    return adjoint_level(middle, winds[0, 0], winds[0, 1], coupling_level)


def reference(terminal_error_derivative, trajectory_advective_shift, layer_interaction_matrix, measured_local_profile_slot, measured_active_tally, measurement_operator_matrix, measured_departure_values):
    layerwise_contributions = lax.map(vertical_layer_traversal, (jnp.transpose(terminal_error_derivative, (1, 0, 2, 3)), jnp.transpose(trajectory_advective_shift, (2, 0, 1, 3, 4)), layer_interaction_matrix))
    analysis_sens = jnp.transpose(layerwise_contributions, (1, 0, 2, 3))
    sectors = jnp.arange(N_LON, dtype=jnp.int32)[:, None]
    slots = jnp.arange(CAP, dtype=jnp.int32)[None, :]

    def one_device(inputs):
        columns, counts, jacobian, innov, owner = inputs
        band = owner % N_LAT
        rows = band * CLAT + columns // CLON
        cells = sectors * CLON + columns % CLON
        picked = analysis_sens[:, :, rows, cells].reshape(PROGNOSTIC_TOTAL * VERTICAL_LAYERS, N_LON, CAP)
        picked = jnp.transpose(picked, (1, 0, 2))
        sens = jnp.sum(jacobian.astype(jnp.float32) * picked, axis=1)
        live = slots < counts[:, None]
        return jnp.where(live, innov * sens, jnp.float32(0.0))

    owners = jnp.arange(N_LON * N_LAT, dtype=jnp.int32)
    obs_impact = lax.map(one_device, (measured_local_profile_slot, measured_active_tally, measurement_operator_matrix, measured_departure_values, owners))
    return analysis_sens, obs_impact
```

```python
import functools

import jax
import jax.numpy as jnp
from jax import lax
from jax.experimental import pallas as pl
from jax.experimental.pallas import tpu as pltpu
from jax.sharding import PartitionSpec as P

MESH = pl.DeviceIdType.MESH
F32 = jnp.float32
BF16 = jnp.bfloat16
CH = 16
SUB = 8


def each(lo, hi, body, unroll=1):
    def step(i, carry):
        body(i)
        return carry

    lax.fori_loop(lo, hi, step, 0, unroll=unroll)


def kernel(
    dims,
    g_ref, wind_ref, lim_ref, slot_ref, m_ref,
    a_ref, s_ref,
    cells, winds, coef, columns, m_in, slot_in, slot_sm, picked, eye2,
    lon_out, lon_in, lat_out, lat_in, edge, ring, halo, sens, sens_in,
    g_sem, w_sem, a_sem, m_send, m_recv, slot_send, slot_recv, local_sem,
    lon_send, lon_recv, lat_send, lat_recv, sens_send, sens_recv,
):
    n_lon, n_lat, fields, levels, rows, lanes, slots = dims
    chunks = levels // CH
    chan = fields * levels
    lon = lax.axis_index("lon")
    lat = lax.axis_index("lat")
    east, west = lax.rem(lon + 1, n_lon), lax.rem(lon + n_lon - 1, n_lon)
    north, south = lax.rem(lat + 1, n_lat), lax.rem(lat + n_lat - 1, n_lat)

    def fetch_first(l):
        c = l // CH
        for f in range(fields):
            pltpu.make_async_copy(
                g_ref.at[f, l], cells.at[:, f * levels + l, :], g_sem.at[c, f]
            ).start()
        for k in range(2):
            pltpu.make_async_copy(
                wind_ref.at[1, k, l], winds.at[k, :, l, :], w_sem.at[c, k]
            ).start()

    def fetch_second(l):
        c = l // CH
        for k in range(2):
            pltpu.make_async_copy(
                wind_ref.at[0, k, l], winds.at[2 + k, :, l, :], w_sem.at[c, 2 + k]
            ).start()

    each(0, levels, fetch_first)
    each(0, levels, fetch_second)

    def wait_g(c):
        for f in range(fields):
            block = cells.at[:, pl.ds(f * levels + c * CH, CH), :]
            pltpu.make_async_copy(block, block, g_sem.at[c, f]).wait()

    def wait_w(c, k):
        block = winds.at[k, :, pl.ds(c * CH, CH), :]
        pltpu.make_async_copy(block, block, w_sem.at[c, k]).wait()

    barrier = pltpu.get_barrier_semaphore()

    def greet(d):
        pl.semaphore_signal(
            barrier, inc=1, device_id={"lon": lax.rem(lon + d, n_lon)}, device_id_type=MESH
        )

    each(1, n_lon, greet)
    for other in (north, south):
        pl.semaphore_signal(barrier, inc=1, device_id={"lat": other}, device_id_type=MESH)
    pl.semaphore_wait(barrier, n_lon - 1 + 2)

    def slot_copy(d):
        peer = lax.rem(lon + d, n_lon)
        return pltpu.make_async_remote_copy(
            src_ref=slot_ref.at[0, pl.ds(peer, 1), :], dst_ref=slot_in.at[d],
            send_sem=slot_send.at[d], recv_sem=slot_recv.at[d],
            device_id={"lon": peer}, device_id_type=MESH,
        )

    def m_copy(d):
        peer = lax.rem(lon + d, n_lon)
        return pltpu.make_async_remote_copy(
            src_ref=m_ref.at[0, peer], dst_ref=m_in.at[d],
            send_sem=m_send.at[d], recv_sem=m_recv.at[d],
            device_id={"lon": peer}, device_id_type=MESH,
        )

    own_slot = pltpu.make_async_copy(
        slot_ref.at[0, pl.ds(lon, 1), :], slot_in.at[0], slot_recv.at[0]
    )
    own_m = pltpu.make_async_copy(m_ref.at[0, lon], m_in.at[0], m_recv.at[0])
    each(1, n_lon, lambda d: slot_copy(d).start())
    own_slot.start()

    def lon_copy(t, c, side):
        return pltpu.make_async_remote_copy(
            src_ref=lon_out.at[t, c], dst_ref=lon_in.at[t, c, side],
            send_sem=lon_send.at[t, c, side], recv_sem=lon_recv.at[t, c, side],
            device_id={"lon": east if side == 0 else west}, device_id_type=MESH,
        )

    def lat_copy(t, c, side):
        return pltpu.make_async_remote_copy(
            src_ref=lat_out.at[t, c, side], dst_ref=lat_in.at[t, c, side],
            send_sem=lat_send.at[t, c, side], recv_sem=lat_recv.at[t, c, side],
            device_id={"lat": north if side == 0 else south}, device_id_type=MESH,
        )

    lane = lax.broadcasted_iota(jnp.int32, (SUB, lanes), 1)
    pair = lane // 2

    def at(f, low):
        return pl.ds(pl.multiple_of(f * levels + low, SUB), SUB)

    def send_edges(t, c):
        lon_out[t, c] = edge[...].astype(BF16)
        for side, row in ((0, rows - 1), (1, 0)):
            w = winds[2 * t + 1, row, pl.ds(c * CH, CH), :]
            for f in range(fields):
                lat_out[t, c, side, f] = (
                    w * cells[row, pl.ds(f * levels + c * CH, CH), :]
                ).astype(BF16)
        for side in range(2):
            lon_copy(t, c, side).start()
            lat_copy(t, c, side).start()

    def first_edges(c):
        wait_g(c)
        wait_w(c, 0)
        wait_w(c, 1)

        def sub(h):
            low = pl.multiple_of(c * CH + h * SUB, SUB)

            def row(i, acc):
                u = winds[0, i, pl.ds(low, SUB), :]
                here = pair == i
                return tuple(
                    jnp.where(here, pltpu.roll(u * cells[i, at(f, low), :], 2 * i + 1, 1), acc[f])
                    for f in range(fields)
                )

            acc = lax.fori_loop(
                0, rows, row, tuple(jnp.zeros((SUB, lanes), F32) for _ in range(fields)), unroll=4
            )
            for f in range(fields):
                edge[f, pl.ds(pl.multiple_of(h * SUB, SUB), SUB), :] = acc[f]

        each(0, CH // SUB, sub)
        send_edges(0, c)

    def advance(t, c, last):
        for side in range(2):
            lon_copy(t, c, side).wait_recv()
            lat_copy(t, c, side).wait_recv()
        if not last:
            wait_w(c, 2)
            wait_w(c, 3)
        lane16 = lax.broadcasted_iota(jnp.int32, (CH, lanes), 1)
        for f in range(fields):
            from_west = lon_in[t, c, 0, f].astype(F32)
            from_east = lon_in[t, c, 1, f].astype(F32)
            ring[f] = jnp.where(
                lane16 % 2 == 1, pltpu.roll(from_west, 1, 1), pltpu.roll(from_east, lanes - 1, 1)
            )
            halo[0, f] = jnp.where(lat == 0, 0.0, lat_in[t, c, 0, f].astype(F32))
            halo[1, f] = jnp.where(lat == n_lat - 1, 0.0, lat_in[t, c, 1, f].astype(F32))

        def sub(h):
            low = pl.multiple_of(c * CH + h * SUB, SUB)
            inner = pl.ds(pl.multiple_of(h * SUB, SUB), SUB)
            k = [[coef[e, f, pl.ds(low, SUB), :] for f in range(fields)] for e in range(fields)]
            rims = [ring[f, inner, :] for f in range(fields)]

            def row(i, below, mid, above, acc):
                g = [cells[i, at(f, low), :] for f in range(fields)]
                u = winds[2 * t, i, pl.ds(low, SUB), :]
                back = lanes - 1 - 2 * i
                fresh = []
                for f in range(fields):
                    p = u * g[f]
                    rim = pltpu.roll(rims[f], back, 1)
                    from_west = jnp.where(lane == 0, rim, pltpu.roll(p, 1, 1))
                    from_east = jnp.where(lane == lanes - 1, rim, pltpu.roll(p, lanes - 1, 1))
                    total = k[0][f] * g[0]
                    for e in range(1, fields):
                        total = total + k[e][f] * g[e]
                    total = total - (from_west - from_east) - (below[f] - above[f])
                    cells[i, at(f, low), :] = total
                    fresh.append(total)
                if last:
                    return acc
                v = winds[2, i, pl.ds(low, SUB), :]
                here = pair == i
                return tuple(
                    jnp.where(here, pltpu.roll(v * fresh[f], 2 * i + 1, 1), acc[f])
                    for f in range(fields)
                )

            def lat_product(i):
                w = winds[2 * t + 1, i, pl.ds(low, SUB), :]
                return tuple(w * cells[i, at(f, low), :] for f in range(fields))

            def step(i, carry):
                below, mid, acc = carry
                above = lat_product(i + 1)
                acc = row(i, below, mid, above, acc)
                return mid, above, acc

            acc = () if last else tuple(jnp.zeros((SUB, lanes), F32) for _ in range(fields))
            below = tuple(halo[0, f, inner, :] for f in range(fields))
            below, mid, acc = lax.fori_loop(
                0, rows - 1, step, (below, lat_product(0), acc), unroll=3
            )
            above = tuple(halo[1, f, inner, :] for f in range(fields))
            acc = row(rows - 1, below, mid, above, acc)
            if not last:
                for f in range(fields):
                    edge[f, inner, :] = acc[f]

        each(0, CH // SUB, sub)
        if not last:
            send_edges(1, c)

    for e in range(fields):
        block = lim_ref[:, e, :]
        for f in range(fields):
            column = block[:, f : f + 1] + (1.0 if e == f else 0.0)
            coef[e, f] = jnp.broadcast_to(column, (levels, lanes))

    at_row = lax.broadcasted_iota(jnp.int32, (lanes, 2 * lanes), 0)
    at_col = lax.broadcasted_iota(jnp.int32, (lanes, 2 * lanes), 1)
    eye2[...] = jnp.where(at_row == at_col % lanes, 1.0, 0.0).astype(BF16)

    each(1, n_lon, lambda d: m_copy(d).start())
    own_m.start()
    each(0, chunks, first_edges)
    each(0, chunks, lambda c: advance(0, c, False))

    def finish(c):
        advance(1, c, True)

        def put(h):
            l = c * CH + h
            for f in range(fields):
                pltpu.make_async_copy(
                    cells.at[:, f * levels + l, :], a_ref.at[f, l], a_sem.at[c, f]
                ).start()

        each(0, CH, put)

    each(0, chunks, finish)

    def turn(i):
        x = cells[i]
        hi = x.astype(BF16)
        lo = (x - hi.astype(F32)).astype(BF16)
        both = jnp.concatenate([hi, lo], axis=1)
        r = lax.dot_general(
            eye2[...], both, (((1,), (1,)), ((), ())), preferred_element_type=F32
        )
        span = pl.ds(pl.multiple_of(i * lanes, lanes), lanes)
        columns[0, span, :] = r[:, :lanes]
        columns[1, span, : chan - lanes] = r[:, lanes:]

    each(0, rows, turn)

    each(1, n_lon, lambda d: slot_copy(d).wait_recv())
    own_slot.wait()
    to_sm = pltpu.make_async_copy(slot_in, slot_sm, local_sem.at[0])
    to_sm.start()
    to_sm.wait()

    def pick(d):
        def some(b):
            for j in range(16):
                n = b * 16 + j
                c = slot_sm[d, 0, n]
                to = d * slots + n
                picked[0, pl.ds(to, 1), :] = columns[0, pl.ds(c, 1), :]
                picked[1, pl.ds(to, 1), :] = columns[1, pl.ds(c, 1), :]

        each(0, slots // 16, some)

    each(0, n_lon, pick)

    eye = lax.broadcasted_iota(jnp.int32, (lanes, lanes), 0) == lax.broadcasted_iota(
        jnp.int32, (lanes, lanes), 1
    )

    def sens_copy(d):
        back = lax.rem(lon + n_lon - d, n_lon)
        return pltpu.make_async_remote_copy(
            src_ref=sens.at[d], dst_ref=sens_in.at[lon],
            send_sem=sens_send.at[d], recv_sem=sens_recv.at[d],
            device_id={"lon": back}, device_id_type=MESH,
        )

    def contract(d):
        for h in range(slots // lanes):
            span = pl.ds(pl.multiple_of(d * slots + h * lanes, lanes), lanes)
            x = jnp.concatenate(
                [picked[0, span, :], picked[1, span, : chan - lanes]], axis=1
            )
            hi = x.astype(BF16)
            lo = (x - hi.astype(F32)).astype(BF16)
            m = m_in[d, :, h * lanes : (h + 1) * lanes]
            r = jnp.dot(hi, m, preferred_element_type=F32) + jnp.dot(
                lo, m, preferred_element_type=F32
            )
            sens[d, :, h * lanes : (h + 1) * lanes] = jnp.sum(
                jnp.where(eye, r, 0.0), axis=0, keepdims=True
            )

    own_m.wait()
    contract(0)
    own_sens = pltpu.make_async_copy(sens.at[0], sens_in.at[lon], sens_recv.at[0])
    own_sens.start()

    def serve(d):
        m_copy(d).wait_recv()
        contract(d)
        sens_copy(d).start()

    each(1, n_lon, serve)

    own_sens.wait()
    each(1, n_lon, lambda d: sens_copy(d).wait_recv())
    s_ref[...] = sens_in[...]

    def drain(d):
        m_copy(d).wait_send()
        slot_copy(d).wait_send()
        sens_copy(d).wait_send()

    each(1, n_lon, drain)

    def drain_chunk(c):
        for t in range(2):
            for side in range(2):
                lon_copy(t, c, side).wait_send()
                lat_copy(t, c, side).wait_send()
        for f in range(fields):
            block = a_ref.at[f, pl.ds(c * CH, CH)]
            pltpu.make_async_copy(block, block, a_sem.at[c, f]).wait()

    each(0, chunks, drain_chunk)


def on_device(sizes, g, wind, lim, slot, tally, operator, departures):
    n_lon, n_lat = sizes
    fields, levels, rows, lanes = g.shape
    slots = slot.shape[2]
    chunks = levels // CH
    chan = fields * levels
    dims = (n_lon, n_lat, fields, levels, rows, lanes, slots)
    dma = pltpu.SemaphoreType.DMA
    anywhere = pl.BlockSpec(memory_space=pl.ANY)
    vmem = pl.BlockSpec(memory_space=pltpu.VMEM)
    analysis, sens = pl.pallas_call(
        functools.partial(kernel, dims),
        out_shape=(
            jax.ShapeDtypeStruct(g.shape, F32),
            jax.ShapeDtypeStruct((n_lon, 1, slots), F32),
        ),
        in_specs=[anywhere, anywhere, vmem, anywhere, anywhere],
        out_specs=(anywhere, vmem),
        scratch_shapes=[
            pltpu.VMEM((rows, chan, lanes), F32),
            pltpu.VMEM((4, rows, levels, lanes), F32),
            pltpu.VMEM((fields, fields, levels, lanes), F32),
            pltpu.VMEM((2, rows * lanes, lanes), F32),
            pltpu.VMEM((n_lon, chan, slots), BF16),
            pltpu.VMEM((n_lon, 1, slots), jnp.int32),
            pltpu.SMEM((n_lon, 1, slots), jnp.int32),
            pltpu.VMEM((2, n_lon * slots, lanes), F32),
            pltpu.VMEM((lanes, 2 * lanes), BF16),
            pltpu.VMEM((2, chunks, fields, CH, lanes), BF16),
            pltpu.VMEM((2, chunks, 2, fields, CH, lanes), BF16),
            pltpu.VMEM((2, chunks, 2, fields, CH, lanes), BF16),
            pltpu.VMEM((2, chunks, 2, fields, CH, lanes), BF16),
            pltpu.VMEM((fields, CH, lanes), F32),
            pltpu.VMEM((fields, CH, lanes), F32),
            pltpu.VMEM((2, fields, CH, lanes), F32),
            pltpu.VMEM((n_lon, 1, slots), F32),
            pltpu.VMEM((n_lon, 1, slots), F32),
            dma((chunks, fields)),
            dma((chunks, 4)),
            dma((chunks, fields)),
            dma((n_lon,)),
            dma((n_lon,)),
            dma((n_lon,)),
            dma((n_lon,)),
            dma((1,)),
            dma((2, chunks, 2)),
            dma((2, chunks, 2)),
            dma((2, chunks, 2)),
            dma((2, chunks, 2)),
            dma((n_lon,)),
            dma((n_lon,)),
        ],
        compiler_params=pltpu.CompilerParams(
            collective_id=0, has_side_effects=True, vmem_limit_bytes=58 << 20
        ),
    )(g, wind, lim, slot, operator)
    live = lax.broadcasted_iota(jnp.int32, (n_lon, slots), 1) < tally[0][:, None]
    impact = jnp.where(live, departures[0] * sens[:, 0], jnp.float32(0.0))[None]
    return analysis, impact


def solution(mesh):
    in_specs = (
        P(None, None, "lat", "lon"),
        P(None, None, None, "lat", "lon"),
        P(),
        P(("lon", "lat"), None, None),
        P(("lon", "lat"), None),
        P(("lon", "lat"), None, None, None),
        P(("lon", "lat"), None, None),
    )
    out_specs = (P(None, None, "lat", "lon"), P(("lon", "lat"), None, None))
    sizes = (mesh.shape["lon"], mesh.shape["lat"])
    return jax.shard_map(
        functools.partial(on_device, sizes),
        mesh=mesh, in_specs=in_specs, out_specs=out_specs, check_vma=False,
    )
```

```python
import functools

import jax
import jax.numpy as jnp
from jax import lax
from jax.experimental import pallas as pl
from jax.experimental.pallas import tpu as pltpu
from jax.sharding import PartitionSpec as P

MESH = pl.DeviceIdType.MESH
F32 = jnp.float32
BF16 = jnp.bfloat16
CH = 16
SUB = 8
GR = 8


def each(lo, hi, body, unroll=1):
    def step(i, carry):
        body(i)
        return carry

    lax.fori_loop(lo, hi, step, 0, unroll=unroll)


def kernel(
    dims,
    g_ref, wind_ref, lim_ref, slot_ref, m_ref,
    a_ref, s_ref,
    cells, winds, coef, columns, m_in, slot_in, slot_sm, picked, eye2, shift,
    lon_out, lon_in, lat_out, lat_in, halo, sens, sens_in,
    g_sem, w_sem, a_sem, m_send, m_recv, slot_send, slot_recv, local_sem,
    lon_send, lon_recv, lat_send, lat_recv, sens_send, sens_recv,
):
    n_lon, n_lat, fields, levels, rows, lanes, slots = dims
    chunks = levels // CH
    chan = fields * levels
    lon = lax.axis_index("lon")
    lat = lax.axis_index("lat")
    east, west = lax.rem(lon + 1, n_lon), lax.rem(lon + n_lon - 1, n_lon)
    north, south = lax.rem(lat + 1, n_lat), lax.rem(lat + n_lat - 1, n_lat)

    def fetch_first(l):
        c = l // CH
        for f in range(fields):
            pltpu.make_async_copy(
                g_ref.at[f, l], cells.at[:, f * levels + l, :], g_sem.at[c, f]
            ).start()
        for k in range(2):
            pltpu.make_async_copy(
                wind_ref.at[1, k, l], winds.at[k, :, l, :], w_sem.at[c, k]
            ).start()

    def fetch_second(l):
        c = l // CH
        for k in range(2):
            pltpu.make_async_copy(
                wind_ref.at[0, k, l], winds.at[2 + k, :, l, :], w_sem.at[c, 2 + k]
            ).start()

    each(0, levels, fetch_first)
    each(0, levels, fetch_second)

    def wait_g(c):
        for f in range(fields):
            block = cells.at[:, pl.ds(f * levels + c * CH, CH), :]
            pltpu.make_async_copy(block, block, g_sem.at[c, f]).wait()

    def wait_w(c, k):
        block = winds.at[k, :, pl.ds(c * CH, CH), :]
        pltpu.make_async_copy(block, block, w_sem.at[c, k]).wait()

    barrier = pltpu.get_barrier_semaphore()

    def greet(d):
        pl.semaphore_signal(
            barrier, inc=1, device_id={"lon": lax.rem(lon + d, n_lon)}, device_id_type=MESH
        )

    each(1, n_lon, greet)
    for other in (north, south):
        pl.semaphore_signal(barrier, inc=1, device_id={"lat": other}, device_id_type=MESH)

    def slot_copy(d):
        peer = lax.rem(lon + d, n_lon)
        return pltpu.make_async_remote_copy(
            src_ref=slot_ref.at[0, pl.ds(peer, 1), :], dst_ref=slot_in.at[d],
            send_sem=slot_send.at[d], recv_sem=slot_recv.at[d],
            device_id={"lon": peer}, device_id_type=MESH,
        )

    def m_copy(d):
        peer = lax.rem(lon + d, n_lon)
        return pltpu.make_async_remote_copy(
            src_ref=m_ref.at[0, peer], dst_ref=m_in.at[d],
            send_sem=m_send.at[d], recv_sem=m_recv.at[d],
            device_id={"lon": peer}, device_id_type=MESH,
        )

    own_slot = pltpu.make_async_copy(
        slot_ref.at[0, pl.ds(lon, 1), :], slot_in.at[0], slot_recv.at[0]
    )
    own_m = pltpu.make_async_copy(m_ref.at[0, lon], m_in.at[0], m_recv.at[0])
    def lon_copy(t, c, side):
        return pltpu.make_async_remote_copy(
            src_ref=lon_out.at[t, c], dst_ref=lon_in.at[t, c, side],
            send_sem=lon_send.at[t, c, side], recv_sem=lon_recv.at[t, c, side],
            device_id={"lon": east if side == 0 else west}, device_id_type=MESH,
        )

    def lat_copy(t, c, side):
        return pltpu.make_async_remote_copy(
            src_ref=lat_out.at[t, c, side], dst_ref=lat_in.at[t, c, side],
            send_sem=lat_send.at[t, c, side], recv_sem=lat_recv.at[t, c, side],
            device_id={"lat": north if side == 0 else south}, device_id_type=MESH,
        )

    def at(f, low):
        return pl.ds(pl.multiple_of(f * levels + low, SUB), SUB)

    def tag(shape, r0, c0, r1, c1, v0, v1):
        r = lax.broadcasted_iota(jnp.int32, shape, 0)
        c = lax.broadcasted_iota(jnp.int32, shape, 1)
        first = jnp.where((r == r0) & (c == c0), v0, 0.0)
        return (first + jnp.where((r == r1) & (c == c1), v1, 0.0)).astype(BF16)

    groups = rows // GR

    def rim_rows(q, b):
        mask = tag((2 * groups, lanes), 2 * b, 0, 2 * b + 1, lanes - 1, 1.0, 1.0)
        return lax.dot_general(
            mask, q.astype(BF16), (((1,), (1,)), ((), ())), preferred_element_type=F32
        )

    def lat_edges(t, c):
        for side, row in ((0, rows - 1), (1, 0)):
            w = winds[2 * t + 1, row, pl.ds(c * CH, CH), :]
            for f in range(fields):
                lat_out[t, c, side, f] = (
                    w * cells[row, pl.ds(f * levels + c * CH, CH), :]
                ).astype(BF16)

    def send_edges(t, c):
        for side in range(2):
            lon_copy(t, c, side).start()
            lat_copy(t, c, side).start()

    def first_edges(c):
        wait_g(c)
        wait_w(c, 0)
        wait_w(c, 1)
        for h in range(CH // SUB):
            low = pl.multiple_of(c * CH + h * SUB, SUB)

            def group(b, acc):
                parts = []
                for r in range(GR):
                    i = b * GR + r
                    u = winds[0, i, pl.ds(low, SUB), :]
                    parts += [u * cells[i, at(f, low), :] for f in range(fields)]
                return acc + rim_rows(jnp.concatenate(parts, axis=0), b)

            acc = lax.fori_loop(
                0, groups, group,
                jnp.zeros((2 * groups, GR * fields * SUB), F32), unroll=8,
            )
            lon_out[0, c, h] = acc.astype(BF16)
        lat_edges(0, c)

    def advance(t, c, last):
        for side in range(2):
            lon_copy(t, c, side).wait_recv()
            lat_copy(t, c, side).wait_recv()
        if not last:
            wait_w(c, 2)
            wait_w(c, 3)
        for f in range(fields):
            halo[0, f] = jnp.where(lat == 0, 0.0, lat_in[t, c, 0, f].astype(F32))
            halo[1, f] = jnp.where(lat == n_lat - 1, 0.0, lat_in[t, c, 1, f].astype(F32))

        def sub(h):
            low = pl.multiple_of(c * CH + h * SUB, SUB)
            inner = pl.ds(pl.multiple_of(h * SUB, SUB), SUB)
            k = [[coef[e, f, pl.ds(low, SUB), :] for f in range(fields)] for e in range(fields)]
            both = jnp.concatenate([lon_in[t, c, 0, h], lon_in[t, c, 1, h]], axis=0)
            rims = jnp.transpose(both.astype(F32)).astype(BF16)

            def lat_product(i):
                w = winds[2 * t + 1, i, pl.ds(low, SUB), :]
                return [w * cells[i, at(f, low), :] for f in range(fields)]

            def group(b, carry):
                below, mid, acc = carry
                base = b * GR
                g = [[cells[base + r, at(f, low), :] for f in range(fields)] for r in range(GR)]
                parts = []
                for r in range(GR):
                    u = winds[2 * t, base + r, pl.ds(low, SUB), :]
                    parts += [u * g[r][f] for f in range(fields)]
                p = jnp.concatenate(parts, axis=0)
                hi = p.astype(BF16)
                lo = (p - hi.astype(F32)).astype(BF16)
                place = tag(
                    (4 * groups, lanes), 2 * b + 1, 0, 2 * groups + 2 * b, lanes - 1, -1.0, 1.0
                )
                lon_term = jnp.dot(
                    jnp.concatenate([hi, lo], axis=1), shift[...], preferred_element_type=F32
                ) + jnp.dot(rims, place, preferred_element_type=F32)
                fresh = []
                for r in range(GR):
                    if r < GR - 1:
                        w = winds[2 * t + 1, base + r + 1, pl.ds(low, SUB), :]
                        above = [w * g[r + 1][f] for f in range(fields)]
                    else:
                        over = b == groups - 1
                        nxt = lat_product(jnp.minimum(base + GR, rows - 1))
                        above = [
                            jnp.where(over, halo[1, f, inner, :], nxt[f]) for f in range(fields)
                        ]
                    for f in range(fields):
                        total = k[0][f] * g[r][0]
                        for e in range(1, fields):
                            total = total + k[e][f] * g[r][e]
                        n = (r * fields + f) * SUB
                        total = total + (above[f] - below[f]) + lon_term[n : n + SUB]
                        cells[base + r, at(f, low), :] = total
                        fresh.append(total)
                    below, mid = mid, above
                if not last:
                    parts = []
                    for r in range(GR):
                        v = winds[2, base + r, pl.ds(low, SUB), :]
                        parts += [v * fresh[r * fields + f] for f in range(fields)]
                    acc = acc + rim_rows(jnp.concatenate(parts, axis=0), b)
                return below, mid, acc

            acc = () if last else jnp.zeros((2 * groups, GR * fields * SUB), F32)
            below = [halo[0, f, inner, :] for f in range(fields)]
            below, mid, acc = lax.fori_loop(
                0, groups, group, (below, lat_product(0), acc), unroll=4
            )
            if not last:
                lon_out[1, c, h] = acc.astype(BF16)

        each(0, CH // SUB, sub)
        if not last:
            lat_edges(1, c)
            send_edges(1, c)

    diag = lax.broadcasted_iota(jnp.int32, (levels, levels), 0) == lax.broadcasted_iota(
        jnp.int32, (levels, levels), 1
    )
    for e in range(fields):
        for f in range(fields):
            line = lim_ref[e, f : f + 1, :] + (1.0 if e == f else 0.0)
            column = jnp.sum(
                jnp.where(diag, jnp.broadcast_to(line, (levels, levels)), 0.0),
                axis=1, keepdims=True,
            )
            coef[e, f] = jnp.broadcast_to(column, (levels, lanes))

    at_row = lax.broadcasted_iota(jnp.int32, (lanes, 2 * lanes), 0)
    at_col = lax.broadcasted_iota(jnp.int32, (lanes, 2 * lanes), 1)
    eye2[...] = jnp.where(at_row == at_col % lanes, 1.0, 0.0).astype(BF16)
    to_row = lax.broadcasted_iota(jnp.int32, (2 * lanes, lanes), 0) % lanes
    to_col = lax.broadcasted_iota(jnp.int32, (2 * lanes, lanes), 1)
    shift[...] = (
        jnp.where(to_row == to_col + 1, 1.0, 0.0) - jnp.where(to_row == to_col - 1, 1.0, 0.0)
    ).astype(BF16)

    each(0, chunks, first_edges)
    pl.semaphore_wait(barrier, n_lon - 1 + 2)
    each(0, chunks, lambda c: send_edges(0, c))
    each(1, n_lon, lambda d: slot_copy(d).start())
    own_slot.start()
    own_m.start()
    share = (n_lon - 1) // (chunks + 1)
    head = n_lon - chunks * (share + 1)
    each(1, head, lambda d: m_copy(d).start())

    def begin(c):
        advance(0, c, False)
        low = head + c * (share + 1)
        each(low, low + share + 1, lambda d: m_copy(d).start())

    each(0, chunks, begin)

    def finish(c):
        advance(1, c, True)

        def put(h):
            l = c * CH + h
            for f in range(fields):
                pltpu.make_async_copy(
                    cells.at[:, f * levels + l, :], a_ref.at[f, l], a_sem.at[c, f]
                ).start()

        each(0, CH, put)

    each(0, chunks, finish)

    flat = columns.reshape(2, rows * lanes, lanes)
    taken = picked.reshape(2, n_lon * slots, lanes)

    def turn(i):
        x = cells[i]
        hi = x.astype(BF16)
        lo = (x - hi.astype(F32)).astype(BF16)
        both = jnp.concatenate([hi, lo], axis=1)
        r = lax.dot_general(
            eye2[...], both, (((1,), (1,)), ((), ())), preferred_element_type=F32
        )
        span = pl.ds(pl.multiple_of(i * lanes, lanes), lanes)
        flat[0, span, :] = r[:, :lanes]
        flat[1, span, : chan - lanes] = r[:, lanes:]

    each(0, rows, turn, unroll=4)

    each(1, n_lon, lambda d: slot_copy(d).wait_recv())
    own_slot.wait()
    to_sm = pltpu.make_async_copy(slot_in, slot_sm, local_sem.at[0])
    to_sm.start()
    to_sm.wait()

    def pick(d):
        def some(b):
            cs = [slot_sm[d, 0, b * 16 + j] for j in range(16)]
            parts = [(columns[0, c], columns[1, c]) for c in cs]
            for j in range(16):
                for q in range(2):
                    picked[q, d * slots + b * 16 + j] = parts[j][q]

        each(0, slots // 16, some)

    each(0, n_lon, pick)

    eye = lax.broadcasted_iota(jnp.int32, (lanes, lanes), 0) == lax.broadcasted_iota(
        jnp.int32, (lanes, lanes), 1
    )

    def sens_copy(d):
        back = lax.rem(lon + n_lon - d, n_lon)
        return pltpu.make_async_remote_copy(
            src_ref=sens.at[d], dst_ref=sens_in.at[lon],
            send_sem=sens_send.at[d], recv_sem=sens_recv.at[d],
            device_id={"lon": back}, device_id_type=MESH,
        )

    def contract(d):
        for h in range(slots // lanes):
            span = pl.ds(pl.multiple_of(d * slots + h * lanes, lanes), lanes)
            x = jnp.concatenate(
                [taken[0, span, :], taken[1, span, : chan - lanes]], axis=1
            )
            hi = x.astype(BF16)
            lo = (x - hi.astype(F32)).astype(BF16)
            m = m_in[d, :, h * lanes : (h + 1) * lanes]
            r = jnp.dot(hi, m, preferred_element_type=F32) + jnp.dot(
                lo, m, preferred_element_type=F32
            )
            sens[d, :, h * lanes : (h + 1) * lanes] = jnp.sum(
                jnp.where(eye, r, 0.0), axis=0, keepdims=True
            )

    own_m.wait()
    each(1, n_lon, lambda d: m_copy(d).wait_recv())
    each(0, n_lon, contract, unroll=4)
    each(1, n_lon, lambda d: sens_copy(d).start())
    own_sens = pltpu.make_async_copy(sens.at[0], sens_in.at[lon], sens_recv.at[0])
    own_sens.start()

    own_sens.wait()
    each(1, n_lon, lambda d: sens_copy(d).wait_recv())
    s_ref[...] = sens_in[:, 0, :]

    def drain(d):
        m_copy(d).wait_send()
        slot_copy(d).wait_send()
        sens_copy(d).wait_send()

    each(1, n_lon, drain)

    def drain_chunk(c):
        for t in range(2):
            for side in range(2):
                lon_copy(t, c, side).wait_send()
                lat_copy(t, c, side).wait_send()
        for f in range(fields):
            block = a_ref.at[f, pl.ds(c * CH, CH)]
            pltpu.make_async_copy(block, block, a_sem.at[c, f]).wait()

    each(0, chunks, drain_chunk)


def hand_over(from_ref, to_ref, sem):
    for f in range(from_ref.shape[0]):
        pltpu.make_async_copy(from_ref.at[f], to_ref.at[f], sem.at[f]).start()
    for f in range(from_ref.shape[0]):
        pltpu.make_async_copy(from_ref.at[f], to_ref.at[f], sem.at[f]).wait()


def on_device(sizes, g, wind, lim, slot, tally, operator, departures):
    n_lon, n_lat = sizes
    fields, levels, rows, lanes = g.shape
    slots = slot.shape[2]
    chunks = levels // CH
    chan = fields * levels
    dims = (n_lon, n_lat, fields, levels, rows, lanes, slots)
    dma = pltpu.SemaphoreType.DMA
    anywhere = pl.BlockSpec(memory_space=pl.ANY)
    vmem = pl.BlockSpec(memory_space=pltpu.VMEM)
    analysis, sens = pl.pallas_call(
        functools.partial(kernel, dims),
        out_shape=(
            pltpu.VMEM(g.shape, F32),
            jax.ShapeDtypeStruct((n_lon, slots), F32),
        ),
        in_specs=[anywhere, anywhere, vmem, anywhere, anywhere],
        out_specs=(vmem, vmem),
        scratch_shapes=[
            pltpu.VMEM((rows, chan, lanes), F32),
            pltpu.VMEM((4, rows, levels, lanes), F32),
            pltpu.VMEM((fields, fields, levels, lanes), F32),
            pltpu.VMEM((2, rows * lanes, 1, lanes), F32),
            pltpu.VMEM((n_lon, chan, slots), BF16),
            pltpu.VMEM((n_lon, 1, slots), jnp.int32),
            pltpu.SMEM((n_lon, 1, slots), jnp.int32),
            pltpu.VMEM((2, n_lon * slots, 1, lanes), F32),
            pltpu.VMEM((lanes, 2 * lanes), BF16),
            pltpu.VMEM((2 * lanes, lanes), BF16),
            pltpu.VMEM((2, chunks, CH // SUB, 2 * rows // GR, GR * fields * SUB), BF16),
            pltpu.VMEM((2, chunks, 2, CH // SUB, 2 * rows // GR, GR * fields * SUB), BF16),
            pltpu.VMEM((2, chunks, 2, fields, CH, lanes), BF16),
            pltpu.VMEM((2, chunks, 2, fields, CH, lanes), BF16),
            pltpu.VMEM((2, fields, CH, lanes), F32),
            pltpu.VMEM((n_lon, 1, slots), F32),
            pltpu.VMEM((n_lon, 1, slots), F32),
            dma((chunks, fields)),
            dma((chunks, 4)),
            dma((chunks, fields)),
            dma((n_lon,)),
            dma((n_lon,)),
            dma((n_lon,)),
            dma((n_lon,)),
            dma((1,)),
            dma((2, chunks, 2)),
            dma((2, chunks, 2)),
            dma((2, chunks, 2)),
            dma((2, chunks, 2)),
            dma((n_lon,)),
            dma((n_lon,)),
        ],
        compiler_params=pltpu.CompilerParams(
            collective_id=0, has_side_effects=True, vmem_limit_bytes=50 << 20
        ),
    )(g, wind, jnp.transpose(lim, (1, 2, 0)), slot, operator)
    analysis = pl.pallas_call(
        hand_over,
        out_shape=jax.ShapeDtypeStruct(g.shape, F32),
        in_specs=[vmem], out_specs=anywhere,
        scratch_shapes=[dma((fields,))],
        compiler_params=pltpu.CompilerParams(vmem_limit_bytes=1 << 20),
    )(pltpu.with_memory_space_constraint(analysis, pltpu.VMEM))
    live = lax.broadcasted_iota(jnp.int32, (n_lon, slots), 1) < tally[0][:, None]
    impact = jnp.where(live, departures[0] * sens, jnp.float32(0.0))[None]
    return analysis, impact


def solution(mesh):
    in_specs = (
        P(None, None, "lat", "lon"),
        P(None, None, None, "lat", "lon"),
        P(),
        P(("lon", "lat"), None, None),
        P(("lon", "lat"), None),
        P(("lon", "lat"), None, None, None),
        P(("lon", "lat"), None, None),
    )
    out_specs = (P(None, None, "lat", "lon"), P(("lon", "lat"), None, None))
    sizes = (mesh.shape["lon"], mesh.shape["lat"])
    return jax.shard_map(
        functools.partial(on_device, sizes),
        mesh=mesh, in_specs=in_specs, out_specs=out_specs, check_vma=False,
    )
```

```python
import functools

import jax
import jax.numpy as jnp
from jax import lax
from jax.experimental import pallas as pl
from jax.experimental.pallas import tpu as pltpu
from jax.sharding import PartitionSpec as P

MESH = pl.DeviceIdType.MESH
F32 = jnp.float32
BF16 = jnp.bfloat16
CH = 16
SUB = 8
GR = 8


def each(lo, hi, body, unroll=1):
    def step(i, carry):
        body(i)
        return carry

    lax.fori_loop(lo, hi, step, 0, unroll=unroll)


def kernel(
    dims,
    g_ref, wind_ref, lim_ref, slot_ref, m_ref,
    a_ref, s_ref,
    cells, winds, coef, columns, m_in, slot_in, slot_sm, picked, eye2, shift,
    lon_out, lon_in, lat_out, lat_in, halo, sens, sens_in,
    g_sem, w_sem, a_sem, m_send, m_recv, slot_send, slot_recv, local_sem,
    lon_send, lon_recv, lat_send, lat_recv, sens_send, sens_recv,
):
    n_lon, n_lat, fields, levels, rows, lanes, slots = dims
    chunks = levels // CH
    chan = fields * levels
    lon = lax.axis_index("lon")
    lat = lax.axis_index("lat")
    east, west = lax.rem(lon + 1, n_lon), lax.rem(lon + n_lon - 1, n_lon)
    north, south = lax.rem(lat + 1, n_lat), lax.rem(lat + n_lat - 1, n_lat)

    def fetch_first(l):
        c = l // CH
        for f in range(fields):
            pltpu.make_async_copy(
                g_ref.at[f, l], cells.at[:, f * levels + l, :], g_sem.at[c, f]
            ).start()
        for k in range(2):
            pltpu.make_async_copy(
                wind_ref.at[1, k, l], winds.at[k, :, l, :], w_sem.at[c, k]
            ).start()

    def fetch_second(l):
        c = l // CH
        for k in range(2):
            pltpu.make_async_copy(
                wind_ref.at[0, k, l], winds.at[2 + k, :, l, :], w_sem.at[c, 2 + k]
            ).start()

    each(0, levels, fetch_first)
    each(0, levels, fetch_second)

    def wait_g(c):
        for f in range(fields):
            block = cells.at[:, pl.ds(f * levels + c * CH, CH), :]
            pltpu.make_async_copy(block, block, g_sem.at[c, f]).wait()

    def wait_w(c, k):
        block = winds.at[k, :, pl.ds(c * CH, CH), :]
        pltpu.make_async_copy(block, block, w_sem.at[c, k]).wait()

    barrier = pltpu.get_barrier_semaphore()

    def greet(d):
        pl.semaphore_signal(
            barrier, inc=1, device_id={"lon": lax.rem(lon + d, n_lon)}, device_id_type=MESH
        )

    each(1, n_lon, greet)
    for other in (north, south):
        pl.semaphore_signal(barrier, inc=1, device_id={"lat": other}, device_id_type=MESH)

    def slot_copy(d):
        peer = lax.rem(lon + d, n_lon)
        return pltpu.make_async_remote_copy(
            src_ref=slot_ref.at[0, pl.ds(peer, 1), :], dst_ref=slot_in.at[d],
            send_sem=slot_send.at[d], recv_sem=slot_recv.at[d],
            device_id={"lon": peer}, device_id_type=MESH,
        )

    def m_copy(d):
        peer = lax.rem(lon + d, n_lon)
        return pltpu.make_async_remote_copy(
            src_ref=m_ref.at[0, peer], dst_ref=m_in.at[d],
            send_sem=m_send.at[d], recv_sem=m_recv.at[d],
            device_id={"lon": peer}, device_id_type=MESH,
        )

    own_slot = pltpu.make_async_copy(
        slot_ref.at[0, pl.ds(lon, 1), :], slot_in.at[0], slot_recv.at[0]
    )
    own_m = pltpu.make_async_copy(m_ref.at[0, lon], m_in.at[0], m_recv.at[0])
    def lon_copy(t, c, side):
        return pltpu.make_async_remote_copy(
            src_ref=lon_out.at[t, c], dst_ref=lon_in.at[t, c, side],
            send_sem=lon_send.at[t, c, side], recv_sem=lon_recv.at[t, c, side],
            device_id={"lon": east if side == 0 else west}, device_id_type=MESH,
        )

    def lat_copy(t, c, side):
        return pltpu.make_async_remote_copy(
            src_ref=lat_out.at[t, c, side], dst_ref=lat_in.at[t, c, side],
            send_sem=lat_send.at[t, c, side], recv_sem=lat_recv.at[t, c, side],
            device_id={"lat": north if side == 0 else south}, device_id_type=MESH,
        )

    def at(f, low):
        return pl.ds(pl.multiple_of(f * levels + low, SUB), SUB)

    def tag(shape, r0, c0, r1, c1, v0, v1):
        r = lax.broadcasted_iota(jnp.int32, shape, 0)
        c = lax.broadcasted_iota(jnp.int32, shape, 1)
        first = jnp.where((r == r0) & (c == c0), v0, 0.0)
        return (first + jnp.where((r == r1) & (c == c1), v1, 0.0)).astype(BF16)

    groups = rows // GR

    def rim_rows(q, b):
        mask = tag((2 * groups, lanes), 2 * b, 0, 2 * b + 1, lanes - 1, 1.0, 1.0)
        return lax.dot_general(
            mask, q.astype(BF16), (((1,), (1,)), ((), ())), preferred_element_type=F32
        )

    def lat_edges(t, c):
        for side, row in ((0, rows - 1), (1, 0)):
            w = winds[2 * t + 1, row, pl.ds(c * CH, CH), :]
            for f in range(fields):
                lat_out[t, c, side, f] = (
                    w * cells[row, pl.ds(f * levels + c * CH, CH), :]
                ).astype(BF16)

    def send_edges(t, c):
        for side in range(2):
            lon_copy(t, c, side).start()
            lat_copy(t, c, side).start()

    def first_edges(c):
        wait_g(c)
        wait_w(c, 0)
        wait_w(c, 1)
        for h in range(CH // SUB):
            low = pl.multiple_of(c * CH + h * SUB, SUB)

            def group(b, acc):
                parts = []
                for r in range(GR):
                    i = b * GR + r
                    u = winds[0, i, pl.ds(low, SUB), :]
                    parts += [u * cells[i, at(f, low), :] for f in range(fields)]
                return acc + rim_rows(jnp.concatenate(parts, axis=0), b)

            acc = lax.fori_loop(
                0, groups, group,
                jnp.zeros((2 * groups, GR * fields * SUB), F32), unroll=8,
            )
            lon_out[0, c, h] = acc.astype(BF16)
        lat_edges(0, c)

    def advance(t, c, last):
        for side in range(2):
            lon_copy(t, c, side).wait_recv()
            lat_copy(t, c, side).wait_recv()
        if not last:
            wait_w(c, 2)
            wait_w(c, 3)
        for f in range(fields):
            halo[0, f] = jnp.where(lat == 0, 0.0, lat_in[t, c, 0, f].astype(F32))
            halo[1, f] = jnp.where(lat == n_lat - 1, 0.0, lat_in[t, c, 1, f].astype(F32))

        def sub(h):
            low = pl.multiple_of(c * CH + h * SUB, SUB)
            inner = pl.ds(h * SUB, SUB)
            k = [[coef[e, f, pl.ds(low, SUB), :] for f in range(fields)] for e in range(fields)]
            both = jnp.concatenate([lon_in[t, c, 0, h], lon_in[t, c, 1, h]], axis=0)
            rims = jnp.transpose(both.astype(F32)).astype(BF16)

            def lat_product(i):
                w = winds[2 * t + 1, i, pl.ds(low, SUB), :]
                return [w * cells[i, at(f, low), :] for f in range(fields)]

            def group(b, carry):
                below, mid, acc = carry
                base = b * GR
                g = [[cells[base + r, at(f, low), :] for f in range(fields)] for r in range(GR)]
                parts = []
                for r in range(GR):
                    u = winds[2 * t, base + r, pl.ds(low, SUB), :]
                    parts += [u * g[r][f] for f in range(fields)]
                p = jnp.concatenate(parts, axis=0)
                hi = p.astype(BF16)
                lo = (p - hi.astype(F32)).astype(BF16)
                place = tag(
                    (4 * groups, lanes), 2 * b + 1, 0, 2 * groups + 2 * b, lanes - 1, -1.0, 1.0
                )
                lon_term = jnp.dot(
                    jnp.concatenate([hi, lo], axis=1), shift[...], preferred_element_type=F32
                ) + jnp.dot(rims, place, preferred_element_type=F32)
                fresh = []
                for r in range(GR):
                    if r < GR - 1:
                        w = winds[2 * t + 1, base + r + 1, pl.ds(low, SUB), :]
                        above = [w * g[r + 1][f] for f in range(fields)]
                    else:
                        over = b == groups - 1
                        nxt = lat_product(jnp.minimum(base + GR, rows - 1))
                        above = [
                            jnp.where(over, halo[1, f, inner, :], nxt[f]) for f in range(fields)
                        ]
                    for f in range(fields):
                        total = k[0][f] * g[r][0]
                        for e in range(1, fields):
                            total = total + k[e][f] * g[r][e]
                        n = (r * fields + f) * SUB
                        total = total + (above[f] - below[f]) + lon_term[n : n + SUB]
                        cells[base + r, at(f, low), :] = total
                        fresh.append(total)
                    below, mid = mid, above
                if not last:
                    parts = []
                    for r in range(GR):
                        v = winds[2, base + r, pl.ds(low, SUB), :]
                        parts += [v * fresh[r * fields + f] for f in range(fields)]
                    acc = acc + rim_rows(jnp.concatenate(parts, axis=0), b)
                return below, mid, acc

            acc = () if last else jnp.zeros((2 * groups, GR * fields * SUB), F32)
            below = [halo[0, f, inner, :] for f in range(fields)]
            below, mid, acc = lax.fori_loop(
                0, groups, group, (below, lat_product(0), acc), unroll=8
            )
            if not last:
                lon_out[1, c, h] = acc.astype(BF16)

        for h in range(CH // SUB):
            sub(h)
        if not last:
            lat_edges(1, c)
            send_edges(1, c)

    diag = lax.broadcasted_iota(jnp.int32, (levels, levels), 0) == lax.broadcasted_iota(
        jnp.int32, (levels, levels), 1
    )
    for e in range(fields):
        for f in range(fields):
            line = lim_ref[e, f : f + 1, :] + (1.0 if e == f else 0.0)
            column = jnp.sum(
                jnp.where(diag, jnp.broadcast_to(line, (levels, levels)), 0.0),
                axis=1, keepdims=True,
            )
            coef[e, f] = jnp.broadcast_to(column, (levels, lanes))

    at_row = lax.broadcasted_iota(jnp.int32, (lanes, 2 * lanes), 0)
    at_col = lax.broadcasted_iota(jnp.int32, (lanes, 2 * lanes), 1)
    eye2[...] = jnp.where(at_row == at_col % lanes, 1.0, 0.0).astype(BF16)
    to_row = lax.broadcasted_iota(jnp.int32, (2 * lanes, lanes), 0) % lanes
    to_col = lax.broadcasted_iota(jnp.int32, (2 * lanes, lanes), 1)
    shift[...] = (
        jnp.where(to_row == to_col + 1, 1.0, 0.0) - jnp.where(to_row == to_col - 1, 1.0, 0.0)
    ).astype(BF16)

    each(0, chunks, first_edges)
    pl.semaphore_wait(barrier, n_lon - 1 + 2)
    each(0, chunks, lambda c: send_edges(0, c))
    each(1, n_lon, lambda d: slot_copy(d).start())
    own_slot.start()
    own_m.start()

    def begin(c):
        advance(0, c, False)

    each(0, chunks, begin)
    each(1, n_lon, lambda d: m_copy(d).start())

    def finish(c):
        advance(1, c, True)

        def put(h):
            l = c * CH + h
            for f in range(fields):
                pltpu.make_async_copy(
                    cells.at[:, f * levels + l, :], a_ref.at[f, l], a_sem.at[c, f]
                ).start()

        each(0, CH, put)

    each(1, n_lon, lambda d: slot_copy(d).wait_recv())
    own_slot.wait()
    to_sm = pltpu.make_async_copy(slot_in, slot_sm, local_sem.at[0])
    to_sm.start()
    each(0, chunks, finish)

    flat = columns.reshape(2, rows * lanes, lanes)
    taken = picked.reshape(2, n_lon * slots, lanes)

    def turn(i):
        x = cells[i]
        hi = x.astype(BF16)
        lo = (x - hi.astype(F32)).astype(BF16)
        both = jnp.concatenate([hi, lo], axis=1)
        r = lax.dot_general(
            eye2[...], both, (((1,), (1,)), ((), ())), preferred_element_type=F32
        )
        span = pl.ds(pl.multiple_of(i * lanes, lanes), lanes)
        flat[0, span, :] = r[:, :lanes]
        flat[1, span, : chan - lanes] = r[:, lanes:]

    each(0, rows, turn, unroll=8)

    to_sm.wait()

    def pick(d):
        def some(b):
            cs = [slot_sm[d, 0, b * 16 + j] for j in range(16)]
            parts = [(columns[0, c], columns[1, c]) for c in cs]
            for j in range(16):
                for q in range(2):
                    picked[q, d * slots + b * 16 + j] = parts[j][q]

        each(0, slots // 16, some, unroll=4)

    each(0, n_lon, pick)

    eye = lax.broadcasted_iota(jnp.int32, (lanes, lanes), 0) == lax.broadcasted_iota(
        jnp.int32, (lanes, lanes), 1
    )

    def sens_copy(d):
        back = lax.rem(lon + n_lon - d, n_lon)
        return pltpu.make_async_remote_copy(
            src_ref=sens.at[d], dst_ref=sens_in.at[lon],
            send_sem=sens_send.at[d], recv_sem=sens_recv.at[d],
            device_id={"lon": back}, device_id_type=MESH,
        )

    def contract(d):
        for h in range(slots // lanes):
            span = pl.ds(pl.multiple_of(d * slots + h * lanes, lanes), lanes)
            x = jnp.concatenate(
                [taken[0, span, :], taken[1, span, : chan - lanes]], axis=1
            )
            hi = x.astype(BF16)
            lo = (x - hi.astype(F32)).astype(BF16)
            m = m_in[d, :, h * lanes : (h + 1) * lanes]
            r = jnp.dot(hi, m, preferred_element_type=F32) + jnp.dot(
                lo, m, preferred_element_type=F32
            )
            sens[d, :, h * lanes : (h + 1) * lanes] = jnp.sum(
                jnp.where(eye, r, 0.0), axis=0, keepdims=True
            )

    own_m.wait()
    contract(0)

    def serve(q):
        for j in range(3):
            m_copy(3 * q + 1 + j).wait_recv()
        for j in range(3):
            contract(3 * q + 1 + j)
        for j in range(3):
            sens_copy(3 * q + 1 + j).start()

    each(0, (n_lon - 1) // 3, serve)
    own_sens = pltpu.make_async_copy(sens.at[0], sens_in.at[lon], sens_recv.at[0])
    own_sens.start()

    own_sens.wait()
    each(1, n_lon, lambda d: sens_copy(d).wait_recv())
    s_ref[...] = sens_in[:, 0, :]

    def drain(d):
        m_copy(d).wait_send()
        slot_copy(d).wait_send()
        sens_copy(d).wait_send()

    each(1, n_lon, drain)

    def drain_chunk(c):
        for t in range(2):
            for side in range(2):
                lon_copy(t, c, side).wait_send()
                lat_copy(t, c, side).wait_send()
        for f in range(fields):
            block = a_ref.at[f, pl.ds(c * CH, CH)]
            pltpu.make_async_copy(block, block, a_sem.at[c, f]).wait()

    each(0, chunks, drain_chunk)


def hand_over(from_ref, to_ref, sem):
    for f in range(from_ref.shape[0]):
        pltpu.make_async_copy(from_ref.at[f], to_ref.at[f], sem.at[f]).start()
    for f in range(from_ref.shape[0]):
        pltpu.make_async_copy(from_ref.at[f], to_ref.at[f], sem.at[f]).wait()


def on_device(sizes, g, wind, lim, slot, tally, operator, departures):
    n_lon, n_lat = sizes
    fields, levels, rows, lanes = g.shape
    slots = slot.shape[2]
    chunks = levels // CH
    chan = fields * levels
    dims = (n_lon, n_lat, fields, levels, rows, lanes, slots)
    dma = pltpu.SemaphoreType.DMA
    anywhere = pl.BlockSpec(memory_space=pl.ANY)
    vmem = pl.BlockSpec(memory_space=pltpu.VMEM)
    analysis, sens = pl.pallas_call(
        functools.partial(kernel, dims),
        out_shape=(
            pltpu.VMEM(g.shape, F32),
            jax.ShapeDtypeStruct((n_lon, slots), F32),
        ),
        in_specs=[anywhere, anywhere, vmem, anywhere, anywhere],
        out_specs=(vmem, vmem),
        scratch_shapes=[
            pltpu.VMEM((rows, chan, lanes), F32),
            pltpu.VMEM((4, rows, levels, lanes), F32),
            pltpu.VMEM((fields, fields, levels, lanes), F32),
            pltpu.VMEM((2, rows * lanes, 1, lanes), F32),
            pltpu.VMEM((n_lon, chan, slots), BF16),
            pltpu.VMEM((n_lon, 1, slots), jnp.int32),
            pltpu.SMEM((n_lon, 1, slots), jnp.int32),
            pltpu.VMEM((2, n_lon * slots, 1, lanes), F32),
            pltpu.VMEM((lanes, 2 * lanes), BF16),
            pltpu.VMEM((2 * lanes, lanes), BF16),
            pltpu.VMEM((2, chunks, CH // SUB, 2 * rows // GR, GR * fields * SUB), BF16),
            pltpu.VMEM((2, chunks, 2, CH // SUB, 2 * rows // GR, GR * fields * SUB), BF16),
            pltpu.VMEM((2, chunks, 2, fields, CH, lanes), BF16),
            pltpu.VMEM((2, chunks, 2, fields, CH, lanes), BF16),
            pltpu.VMEM((2, fields, CH, lanes), F32),
            pltpu.VMEM((n_lon, 1, slots), F32),
            pltpu.VMEM((n_lon, 1, slots), F32),
            dma((chunks, fields)),
            dma((chunks, 4)),
            dma((chunks, fields)),
            dma((n_lon,)),
            dma((n_lon,)),
            dma((n_lon,)),
            dma((n_lon,)),
            dma((1,)),
            dma((2, chunks, 2)),
            dma((2, chunks, 2)),
            dma((2, chunks, 2)),
            dma((2, chunks, 2)),
            dma((n_lon,)),
            dma((n_lon,)),
        ],
        compiler_params=pltpu.CompilerParams(
            collective_id=0, has_side_effects=True, vmem_limit_bytes=50 << 20
        ),
    )(g, wind, jnp.transpose(lim, (1, 2, 0)), slot, operator)
    analysis = pl.pallas_call(
        hand_over,
        out_shape=jax.ShapeDtypeStruct(g.shape, F32),
        in_specs=[vmem], out_specs=anywhere,
        scratch_shapes=[dma((fields,))],
        compiler_params=pltpu.CompilerParams(vmem_limit_bytes=1 << 20),
    )(pltpu.with_memory_space_constraint(analysis, pltpu.VMEM))
    live = lax.broadcasted_iota(jnp.int32, (n_lon, slots), 1) < tally[0][:, None]
    impact = jnp.where(live, departures[0] * sens, jnp.float32(0.0))[None]
    return analysis, impact


def solution(mesh):
    in_specs = (
        P(None, None, "lat", "lon"),
        P(None, None, None, "lat", "lon"),
        P(),
        P(("lon", "lat"), None, None),
        P(("lon", "lat"), None),
        P(("lon", "lat"), None, None, None),
        P(("lon", "lat"), None, None),
    )
    out_specs = (P(None, None, "lat", "lon"), P(("lon", "lat"), None, None))
    sizes = (mesh.shape["lon"], mesh.shape["lat"])
    return jax.shard_map(
        functools.partial(on_device, sizes),
        mesh=mesh, in_specs=in_specs, out_specs=out_specs, check_vma=False,
    )
```
